32 devices in a mesh: groups: 2 (over y), wave: 4 (over z), section: 4 (over x, core).
Axes of the slice: x: 2, y: 2, z: 4, core: 2. Of those that a mesh axis runs over, the one named last changes fastest.
Arguments:
- nominal_field: float32 [4, 2, 1024], P('wave'), may hold values from -6 to 6
- sensitivity: bfloat16 [4, 360, 2, 1024], P('wave'), may hold values from -0.3125 to 0.3125
- aberrations: bfloat16 [128, 360], P('groups'), parts along dimension 0, may hold values from -13 to 13
- jacobian: bfloat16 [4, 2, 1024, 8192], P('wave', None, None, 'section'), may hold values from -1 to 1
- tile_mask: int32 [4, 8], P('wave'), may hold values 0 or 1
- regul: float32 [8192], P('section'), may hold values from 0.05 to 0.5
- initial_commands: float32 [128, 8192], P('groups', 'section'), parts along dimension 0, may hold values from -3 to 3
Outputs:
- commands: float32 [128, 8192], P('groups', 'section'), parts along dimension 0
- dark_field: float32 [128, 4, 2, 1024], P('groups', 'wave'), parts along dimension 0
The draws below stay inside these ranges and needn't reach their ends.
There are 2 independent parts, one for each index of `groups`. The reference program is written for one: setup_inputs(seed, part) draws one part's arguments, and reference() takes and returns one part's arrays. A program takes and returns all parts, laid end to end along the dimension named above; an argument that names none is the same for every part. Nothing has to cross between parts.
All inputs are finite; a program needn't handle non-finite values. No bound on the sum of `tile_mask` on one device may be relied on, other than what follows from the above.
Results may differ from the reference program's by a relative error of at most 0.035.
Values may be sent and summed in bfloat16 or wider, within the bound.
A program may use at most 64 MiB of HBM per device.

```python
import math
import jax
import jax.numpy as jnp
from jax import lax

ACT = 8192
MODES = 360
TILE = 128
TILES = 8
ITERS = 2
CG = 5
PIX = 1024
REALS = 64
WAVES = 4
ACT_DEV = 2048
N_SECTION = 4


def draw_jacobian(key, part):
    column = jnp.arange(ACT, dtype=jnp.float32) / ACT
    raw = jnp.clip(jax.random.normal(key, (WAVES, 2, PIX, ACT), jnp.float32), -4.0, 4.0)
    scale = 10.0 ** (column - 0.5)
    return jnp.clip(raw * scale * ACT ** (-0.5), -1.0, 1.0).astype(jnp.bfloat16)


def draw_aberrations(key, part):
    first_key, second_key = jax.random.split(jax.random.fold_in(key, 7))
    level = jax.random.uniform(first_key, (REALS, 1), jnp.float32, -0.5, 0.5)
    raw = jnp.clip(jax.random.normal(second_key, (REALS, MODES), jnp.float32), -4.0, 4.0)
    scale = 10.0 ** level
    return (raw * scale).astype(jnp.bfloat16)


def touch_ends(values, rng, smallest, largest):
    index_at = [jax.random.randint(jax.random.fold_in(rng, axis), (), 0, length) for axis, length in enumerate(values.shape)]
    longest = values.shape.index(max(values.shape))
    next_to = index_at[:longest] + [(index_at[longest] + 1) % values.shape[longest]] + index_at[longest + 1:]
    return values.at[tuple(index_at)].set(smallest).at[tuple(next_to)].set(largest)


def level_of(own_key, shape, cuts, low, largest):
    level = 1.0
    for axis_at, parts in cuts:
        heights = jax.random.uniform(jax.random.fold_in(jax.random.fold_in(own_key, 6), axis_at), (parts,), jnp.float32, low / len(cuts), largest / len(cuts))
        level = level * jnp.repeat(jnp.exp(heights), shape[axis_at] // parts).reshape((-1,) + (1,) * (len(shape) - 1 - axis_at))
    return level


def scatter_about(rng, extent, deviation, limit, cuts=(), kind=jnp.bfloat16):
    level = level_of(rng, extent, cuts, -0.22, 0.18) if cuts else 1.0
    values = jax.random.normal(rng, extent, jnp.float32) * deviation * level
    return jnp.minimum(jnp.maximum(values, -limit), limit).astype(kind)


def setup_inputs(seed: int = 0, part: int = 0) -> dict:
    arg_keys = jax.random.split(jax.random.key(seed), 8)
    part_keys = jax.random.split(jax.random.fold_in(arg_keys[7], part), 8)
    return {
        "nominal_field": scatter_about(arg_keys[0], (WAVES, 2, PIX), 1.0, 6.0, ((0, 4),), jnp.float32),
        "sensitivity": scatter_about(arg_keys[1], (WAVES, MODES, 2, PIX), MODES ** -0.5, 0.3125, ((0, 4),)),
        "aberrations": draw_aberrations(jax.random.fold_in(jax.random.fold_in(arg_keys[7], part), 71), part),
        "jacobian": draw_jacobian(jax.random.fold_in(arg_keys[7], 71), part),
        "tile_mask": touch_ends((jax.random.randint(arg_keys[4], (WAVES, TILES), 0, 4) < 3).astype(jnp.int32), jax.random.fold_in(arg_keys[4], 1), 0, 1),
        "regul": jnp.clip(jnp.exp(math.log(0.5) - 2.3025851 * jax.random.uniform(arg_keys[5], (ACT,), jnp.float32) ** level_of(arg_keys[5], (ACT,), ((0, 4),), -0.2, 0.2)), 0.05, 0.5),
        "initial_commands": scatter_about(part_keys[6], (REALS, ACT), 0.5, 3.0, ((1, 4),), jnp.float32),
    }


epsilon = 1e-6


def image_of(command_bf, flat_jac):
    def advance(total_sum, block_index):
        offset = block_index * ACT_DEV
        jac_cols = lax.dynamic_slice_in_dim(flat_jac, offset, ACT_DEV, 1)
        command_cols = lax.dynamic_slice_in_dim(command_bf, offset, ACT_DEV, 1)
        partial_value = jnp.dot(command_cols, jac_cols.T, preferred_element_type=jnp.float32)
        partial_value = lax.optimization_barrier(partial_value.astype(jnp.bfloat16)).astype(jnp.float32)
        return total_sum + partial_value, None

    start_sum = jnp.zeros((command_bf.shape[0], flat_jac.shape[0]), jnp.float32)
    result, _ = lax.scan(advance, start_sum, jnp.arange(N_SECTION, dtype=jnp.int32))
    return result


def back_of(masked_bf, flat_jac):
    span = 2 * PIX

    def advance(total_sum, wave_index):
        offset = wave_index * span
        jac_rows = lax.dynamic_slice_in_dim(flat_jac, offset, span, 0)
        field_rows = lax.dynamic_slice_in_dim(masked_bf, offset, span, 1)
        partial_value = jnp.dot(field_rows, jac_rows, preferred_element_type=jnp.float32)
        partial_value = lax.optimization_barrier(partial_value.astype(jnp.bfloat16)).astype(jnp.float32)
        return total_sum + partial_value, None

    start_sum = jnp.zeros((masked_bf.shape[0], ACT), jnp.float32)
    result, _ = lax.scan(advance, start_sum, jnp.arange(WAVES, dtype=jnp.int32))
    return result


def reference(nominal_field, sensitivity, aberrations, jacobian, tile_mask, regul, initial_commands):
    rows_all = WAVES * 2 * PIX
    flat_jac = jacobian.reshape(rows_all, ACT)
    weight = jnp.broadcast_to(tile_mask.astype(jnp.float32)[:, None, :, None], (WAVES, 2, TILES, TILE)).reshape(1, rows_all)
    sens_rows = jnp.transpose(sensitivity, (1, 0, 2, 3)).reshape(MODES, rows_all)
    field_now = nominal_field.reshape(1, rows_all) + jnp.dot(aberrations, sens_rows, preferred_element_type=jnp.float32)
    commands = initial_commands
    field_now = field_now + image_of(commands.astype(jnp.bfloat16), flat_jac)
    for iteration in range(ITERS):
        residual = -back_of((weight * field_now).astype(jnp.bfloat16), flat_jac)
        direction = residual
        change = jnp.zeros_like(residual)
        field_step = jnp.zeros_like(field_now)
        norm_now = jnp.sum(residual * residual, axis=1)
        for inner_step in range(CG):
            image_now = image_of(direction.astype(jnp.bfloat16), flat_jac)
            applied = back_of((weight * image_now).astype(jnp.bfloat16), flat_jac) + regul[None, :] * direction
            curvature = jnp.sum(direction * applied, axis=1)
            step_len = norm_now / (curvature + epsilon)
            change = change + step_len[:, None] * direction
            field_step = field_step + step_len[:, None] * image_now
            residual = residual - step_len[:, None] * applied
            norm_next = jnp.sum(residual * residual, axis=1)
            direction = residual + (norm_next / (norm_now + epsilon))[:, None] * direction
            norm_now = norm_next
        commands = commands + change
        field_now = field_now + field_step
    return commands, field_now.reshape(REALS, WAVES, 2, PIX)
```

```python
import functools

import jax
import jax.numpy as jnp
from jax import lax
from jax.experimental import pallas as pl
from jax.experimental.pallas import tpu as pltpu
from jax.sharding import PartitionSpec as P

ITERS = 2
CG = 5
LANES = 128
CHUNKS = 2

epsilon = 1e-06


def to_section_image(command_bf, jac_block):
    partial_value = lax.dot_general(
        command_bf, jac_block, (((1,), (1,)), ((), ())), preferred_element_type=jnp.float32
    )
    return lax.psum_scatter(
        partial_value.astype(jnp.bfloat16), "section", scatter_dimension=1, tiled=True
    ).astype(jnp.float32)


def back_of(masked_share, jac_block):
    masked_bf = lax.all_gather(masked_share, "section", axis=1, tiled=True)
    partial_value = jnp.dot(masked_bf, jac_block, preferred_element_type=jnp.float32)
    owned = lax.psum_scatter(
        partial_value.astype(jnp.bfloat16), "wave", scatter_dimension=1, tiled=True
    ).astype(jnp.float32)
    return lax.all_gather(owned, "wave", axis=1, tiled=True)


def reduce_scalars(values):
    return lax.psum(values, "section")


def general_shards(nominal_field, sensitivity, aberrations, jacobian, tile_mask, regul, initial_commands):
    components = jacobian.shape[1]
    pixels = jacobian.shape[2]
    block_width = jacobian.shape[3]
    row_count = components * pixels
    share_rows = row_count // lax.axis_size("section")
    row_start = lax.axis_index("section") * share_rows
    jac_block = jacobian.reshape(row_count, block_width)
    tile_count = tile_mask.shape[1]
    weight_full = jnp.broadcast_to(
        tile_mask[0].astype(jnp.float32)[None, :, None],
        (components, tile_count, pixels // tile_count),
    ).reshape(1, row_count)
    weight = lax.dynamic_slice_in_dim(weight_full, row_start, share_rows, 1)
    mode_count = sensitivity.shape[1]
    sens_share = lax.dynamic_slice_in_dim(
        sensitivity.reshape(mode_count, row_count), row_start, share_rows, 1
    )
    nominal_share = lax.dynamic_slice_in_dim(
        nominal_field.reshape(1, row_count), row_start, share_rows, 1
    )
    field_now = nominal_share + jnp.dot(aberrations, sens_share, preferred_element_type=jnp.float32)
    commands = initial_commands
    field_now = field_now + to_section_image(commands.astype(jnp.bfloat16), jac_block)
    for iteration in range(ITERS):
        residual = -back_of((weight * field_now).astype(jnp.bfloat16), jac_block)
        direction = residual
        change = jnp.zeros_like(residual)
        field_step = jnp.zeros_like(field_now)
        norm_now = reduce_scalars(jnp.sum(residual * residual, axis=1))
        for inner_step in range(CG):
            image_now = to_section_image(direction.astype(jnp.bfloat16), jac_block)
            applied = (
                back_of((weight * image_now).astype(jnp.bfloat16), jac_block)
                + regul[None, :] * direction
            )
            curvature = reduce_scalars(jnp.sum(direction * applied, axis=1))
            step_len = norm_now / (curvature + epsilon)
            residual = residual - step_len[:, None] * applied
            norm_next = reduce_scalars(jnp.sum(residual * residual, axis=1))
            change = change + step_len[:, None] * direction
            field_step = field_step + step_len[:, None] * image_now
            direction = residual + (norm_next / (norm_now + epsilon))[:, None] * direction
            norm_now = norm_next
        commands = commands + change
        field_now = field_now + field_step
    whole_field = lax.all_gather(
        field_now.astype(jnp.bfloat16), "section", axis=1, tiled=True
    ).astype(field_now.dtype)
    return (commands, whole_field.reshape(whole_field.shape[0], 1, components, pixels))


def control_kernel(
    n,
    rb,
    jac_hbm,
    base_ref,
    start_ref,
    regul_ref,
    weight_ref,
    cmd_ref,
    out_ref,
    jac,
    probe,
    masked,
    sec_part,
    sec_recv,
    wav_part,
    wav_recv,
    image,
    field,
    residual,
    direction,
    acc,
    dots_send,
    dots_recv,
    norm,
    steps,
    jac_sem,
    sec_ss,
    sec_rs,
    msk_ss,
    msk_rs,
    wav_ss,
    wav_rs,
    prb_ss,
    prb_rs,
    dot_ss,
    dot_rs,
    stp_ss,
    stp_rs,
):
    f32, bf16 = jnp.float32, jnp.bfloat16
    rows, acts = jac.shape
    reals = n * rb
    rc, ac = rows // CHUNKS, acts // CHUNKS
    sec, wav = lax.axis_index("section"), lax.axis_index("wave")
    sec_peer = [lax.rem(sec + k, n) for k in range(1, n)]
    wav_peer = [lax.rem(wav + k, n) for k in range(1, n)]

    load = pltpu.make_async_copy(jac_hbm, jac, jac_sem)
    load.start()
    barrier = pltpu.get_barrier_semaphore()
    for p in sec_peer:
        pl.semaphore_signal(
            barrier, inc=1, device_id={"section": p}, device_id_type=pl.DeviceIdType.MESH
        )
    for p in wav_peer:
        pl.semaphore_signal(
            barrier, inc=1, device_id={"wave": p}, device_id_type=pl.DeviceIdType.MESH
        )
    pl.semaphore_wait(barrier, 2 * (n - 1))

    def to_section(k, src, dst, ss, rs):
        return pltpu.make_async_remote_copy(
            src_ref=src, dst_ref=dst, send_sem=ss, recv_sem=rs,
            device_id={"section": sec_peer[k]}, device_id_type=pl.DeviceIdType.MESH,
        )

    def to_wave(k, src, dst, ss, rs):
        return pltpu.make_async_remote_copy(
            src_ref=src, dst_ref=dst, send_sem=ss, recv_sem=rs,
            device_id={"wave": wav_peer[k]}, device_id_type=pl.DeviceIdType.MESH,
        )

    peers = range(n - 1)

    def sec_copy(j, k):
        return to_section(k, sec_part.at[j, sec_peer[k]], sec_recv.at[j, k], sec_ss.at[j, k], sec_rs.at[j, k])

    def msk_copy(j, k):
        return to_section(k, masked.at[j, sec], masked.at[j, sec], msk_ss.at[j, k], msk_rs.at[j, k])

    def wav_copy(c, k):
        return to_wave(k, wav_part.at[c, wav_peer[k]], wav_recv.at[c, k], wav_ss.at[c, k], wav_rs.at[c, k])

    def prb_copy(slot, c, k):
        return to_wave(
            k, probe.at[slot, c, wav], probe.at[slot, c, wav], prb_ss.at[c, k], prb_rs.at[c, k]
        )

    def dot_copy(k):
        return to_section(k, dots_send, dots_recv.at[k], dot_ss.at[k], dot_rs.at[k])

    def stp_copy(k):
        return to_wave(k, steps.at[wav], steps.at[wav], stp_ss.at[k], stp_rs.at[k])

    def make_image(slot, arrive):
        for c in range(CHUNKS):
            arrive(c)
            lhs = probe[slot, c].reshape(reals, ac)
            for j in range(CHUNKS):
                part = lax.dot_general(
                    lhs,
                    jac[j * rc:(j + 1) * rc, c * ac:(c + 1) * ac],
                    (((1,), (1,)), ((), ())),
                    preferred_element_type=f32,
                )
                if c:
                    part = acc[:, j * rc:(j + 1) * rc] + part
                if c < CHUNKS - 1:
                    acc[:, j * rc:(j + 1) * rc] = part
                else:
                    sec_part[j] = part.astype(bf16).reshape(n, rb, rc)
                    for k in peers:
                        sec_copy(j, k).start()

    def take_image(j):
        for k in peers:
            sec_copy(j, k).wait()
        total = sec_part[j, sec].astype(f32)
        for k in peers:
            total = total + sec_recv[j, k].astype(f32)
        return total

    def send_masked(j, values):
        masked[j, sec] = (weight_ref[:, j * rc:(j + 1) * rc] * values).astype(bf16)
        for k in peers:
            msk_copy(j, k).start()

    def make_back():
        for j in range(CHUNKS):
            for k in peers:
                msk_copy(j, k).wait()
            lhs = masked[j].reshape(reals, rc)
            for c in range(CHUNKS):
                part = jnp.dot(
                    lhs,
                    jac[j * rc:(j + 1) * rc, c * ac:(c + 1) * ac],
                    preferred_element_type=f32,
                )
                if j:
                    part = acc[:, c * ac:(c + 1) * ac] + part
                if j < CHUNKS - 1:
                    acc[:, c * ac:(c + 1) * ac] = part
                else:
                    wav_part[c] = part.astype(bf16).reshape(n, rb, ac)
                    for k in peers:
                        wav_copy(c, k).start()

    def take_back(c):
        for k in peers:
            wav_copy(c, k).wait()
        total = wav_part[c, wav].astype(f32)
        for k in peers:
            total = total + wav_recv[c, k].astype(f32)
        return total

    lane = lax.broadcasted_iota(jnp.int32, (rb, LANES), 1)

    def reduce_dots(values):
        packed = jnp.zeros((rb, LANES), f32)
        for at, value in enumerate(values):
            packed = jnp.where(lane == at, value, packed)
        dots_send[...] = packed
        for k in peers:
            dot_copy(k).start()
        for k in peers:
            dot_copy(k).wait()
        total = dots_send[...]
        for k in peers:
            total = total + dots_recv[k]
        return [total[:, at:at + 1] for at in range(len(values))]

    def row_sum(values):
        return jnp.sum(values, axis=1, keepdims=True)

    def send_probe(slot, c, values):
        probe[slot, c, wav] = values.astype(bf16)
        for k in peers:
            prb_copy(slot, c, k).start()

    def take_steps(slot):
        for k in peers:
            stp_copy(k).wait()
        for j in range(CHUNKS):
            field[j] = field[j] + steps[sec][:, 0:1] * image[j]
        column = steps[...].reshape(reals, LANES)[:, 0:1]
        for c in range(CHUNKS):
            cols = slice(c * ac, (c + 1) * ac)
            cmd_ref[:, cols] = cmd_ref[:, cols] + column * probe[slot, c].reshape(reals, ac).astype(f32)

    cmd_ref[...] = start_ref[...]
    for c in range(CHUNKS):
        probe[0, c] = start_ref[:, c * ac:(c + 1) * ac].astype(bf16).reshape(n, rb, ac)
    load.wait()
    make_image(0, lambda c: None)
    for j in range(CHUNKS):
        field[j] = base_ref[:, j * rc:(j + 1) * rc] + take_image(j)

    def iteration(_, carry):
        for j in range(CHUNKS):
            send_masked(j, field[j])
        make_back()
        square = jnp.zeros((rb, 1), f32)
        for c in range(CHUNKS):
            start = -take_back(c)
            residual[c] = start
            direction[c] = start
            send_probe(0, c, start)
            square = square + row_sum(start * start)
        (first,) = reduce_dots([square])
        norm[...] = jnp.broadcast_to(first, (rb, LANES))

        def cg_step(step, carry):
            slot = lax.rem(step, 2)

            def arrive(c):
                for k in peers:
                    prb_copy(slot, c, k).wait()

            make_image(slot, arrive)

            @pl.when(step > 0)
            def _():
                take_steps(1 - slot)

            for j in range(CHUNKS):
                total = take_image(j)
                image[j] = total
                send_masked(j, total)
            make_back()
            dd = jnp.zeros((rb, 1), f32)
            ra, aa = dd, dd
            for c in range(CHUNKS):
                along = direction[c]
                applied = take_back(c) + regul_ref[:, c * ac:(c + 1) * ac] * along
                acc[0:rb, c * ac:(c + 1) * ac] = applied
                dd = dd + row_sum(along * applied)
                ra = ra + row_sum(residual[c] * applied)
                aa = aa + row_sum(applied * applied)
            curvature, ra, aa = reduce_dots([dd, ra, aa])
            norm_now = norm[:, 0:1]
            step_len = norm_now / (curvature + epsilon)
            norm_next = jnp.maximum(norm_now + step_len * (step_len * aa - 2.0 * ra), 0.0)
            ratio = norm_next / (norm_now + epsilon)
            norm[...] = jnp.broadcast_to(norm_next, (rb, LANES))
            steps[wav] = jnp.broadcast_to(step_len, (rb, LANES))
            for k in peers:
                stp_copy(k).start()

            @pl.when(step < CG - 1)
            def _():
                for c in range(CHUNKS):
                    after = residual[c] - step_len * acc[0:rb, c * ac:(c + 1) * ac]
                    residual[c] = after
                    ahead = after + ratio * direction[c]
                    direction[c] = ahead
                    send_probe(1 - slot, c, ahead)

            return carry

        lax.fori_loop(0, CG, cg_step, 0)
        take_steps((CG - 1) % 2)
        return carry

    lax.fori_loop(0, ITERS, iteration, 0)

    for j in range(CHUNKS):
        masked[j, sec] = field[j].astype(bf16)
        for k in peers:
            msk_copy(j, k).start()
    for j in range(CHUNKS):
        for k in peers:
            msk_copy(j, k).wait()
        out_ref[:, j * rc:(j + 1) * rc] = masked[j].reshape(reals, rc).astype(f32)


def kernel_shards(nominal_field, sensitivity, aberrations, jacobian, tile_mask, regul, initial_commands):
    f32, bf16 = jnp.float32, jnp.bfloat16
    components, pixels, acts = jacobian.shape[1:]
    rows = components * pixels
    reals = initial_commands.shape[0]
    n = lax.axis_size("section")
    rb = reals // n
    rc, ac = rows // CHUNKS, acts // CHUNKS
    tile_count = tile_mask.shape[1]
    weight = jnp.broadcast_to(
        tile_mask[0].astype(f32)[None, :, None],
        (components, tile_count, pixels // tile_count),
    ).reshape(1, rows)
    own = lax.dynamic_slice_in_dim(aberrations, lax.axis_index("section") * rb, rb, 0)
    base = nominal_field[0][None] + lax.dot_general(
        own, sensitivity[0], (((1,), (0,)), ((), ())), preferred_element_type=f32
    )
    vmem = pl.BlockSpec(memory_space=pltpu.VMEM)
    dma = pltpu.SemaphoreType.DMA
    commands, field = pl.pallas_call(
        functools.partial(control_kernel, n, rb),
        out_shape=(
            jax.ShapeDtypeStruct((reals, acts), f32),
            jax.ShapeDtypeStruct((reals, rows), f32),
        ),
        in_specs=[pl.BlockSpec(memory_space=pl.ANY), vmem, vmem, vmem, vmem],
        out_specs=(vmem, vmem),
        scratch_shapes=[
            pltpu.VMEM((rows, acts), bf16),
            pltpu.VMEM((2, CHUNKS, n, rb, ac), bf16),
            pltpu.VMEM((CHUNKS, n, rb, rc), bf16),
            pltpu.VMEM((CHUNKS, n, rb, rc), bf16),
            pltpu.VMEM((CHUNKS, n - 1, rb, rc), bf16),
            pltpu.VMEM((CHUNKS, n, rb, ac), bf16),
            pltpu.VMEM((CHUNKS, n - 1, rb, ac), bf16),
            pltpu.VMEM((CHUNKS, rb, rc), f32),
            pltpu.VMEM((CHUNKS, rb, rc), f32),
            pltpu.VMEM((CHUNKS, rb, ac), f32),
            pltpu.VMEM((CHUNKS, rb, ac), f32),
            pltpu.VMEM((reals, max(rows, acts)), f32),
            pltpu.VMEM((rb, LANES), f32),
            pltpu.VMEM((n - 1, rb, LANES), f32),
            pltpu.VMEM((rb, LANES), f32),
            pltpu.VMEM((n, rb, LANES), f32),
            dma(()),
        ]
        + [dma((CHUNKS, n - 1))] * 8
        + [dma((n - 1,))] * 4,
        compiler_params=pltpu.CompilerParams(
            collective_id=0, has_side_effects=True, vmem_limit_bytes=40 * 1024 * 1024
        ),
        name="control_loop",
    )(
        jacobian.reshape(rows, acts),
        base.reshape(rb, rows),
        initial_commands,
        regul[None, :],
        weight,
    )
    return commands, field.reshape(reals, 1, components, pixels)


def solution(mesh):
    placed = (
        P("wave", None, None),
        P("wave", None, None, None),
        P("groups", None),
        P("wave", None, None, "section"),
        P("wave", None),
        P("section"),
        P("groups", "section"),
    )

    def choose(*args):
        n, waves = mesh.shape["section"], mesh.shape["wave"]
        reals = args[6].shape[0]
        acts = args[3].shape[3]
        rows = args[3].shape[1] * args[3].shape[2]
        fits = (
            n == waves
            and n > 1
            and reals % (16 * n) == 0
            and acts % (LANES * CHUNKS) == 0
            and rows % (LANES * CHUNKS) == 0
            and rows * acts <= 2048 * 2048
            and reals <= 64
        )
        return (kernel_shards if fits else general_shards)(*args)

    return jax.shard_map(
        choose,
        mesh=mesh,
        in_specs=placed,
        out_specs=(P("groups", "section"), P("groups", "wave", None, None)),
        check_vma=False,
    )
```

```python
import functools

import jax
import jax.numpy as jnp
from jax import lax
from jax.experimental import pallas as pl
from jax.experimental.pallas import tpu as pltpu
from jax.sharding import PartitionSpec as P

ITERS = 2
CG = 5
LANES = 128
CHUNKS = 2
STREAMS = 2

epsilon = 1e-06


def to_section_image(command_bf, jac_block):
    partial_value = lax.dot_general(
        command_bf, jac_block, (((1,), (1,)), ((), ())), preferred_element_type=jnp.float32
    )
    return lax.psum_scatter(
        partial_value.astype(jnp.bfloat16), "section", scatter_dimension=1, tiled=True
    ).astype(jnp.float32)


def back_of(masked_share, jac_block):
    masked_bf = lax.all_gather(masked_share, "section", axis=1, tiled=True)
    partial_value = jnp.dot(masked_bf, jac_block, preferred_element_type=jnp.float32)
    owned = lax.psum_scatter(
        partial_value.astype(jnp.bfloat16), "wave", scatter_dimension=1, tiled=True
    ).astype(jnp.float32)
    return lax.all_gather(owned, "wave", axis=1, tiled=True)


def reduce_scalars(values):
    return lax.psum(values, "section")


def general_shards(nominal_field, sensitivity, aberrations, jacobian, tile_mask, regul, initial_commands):
    components = jacobian.shape[1]
    pixels = jacobian.shape[2]
    block_width = jacobian.shape[3]
    row_count = components * pixels
    share_rows = row_count // lax.axis_size("section")
    row_start = lax.axis_index("section") * share_rows
    jac_block = jacobian.reshape(row_count, block_width)
    tile_count = tile_mask.shape[1]
    weight_full = jnp.broadcast_to(
        tile_mask[0].astype(jnp.float32)[None, :, None],
        (components, tile_count, pixels // tile_count),
    ).reshape(1, row_count)
    weight = lax.dynamic_slice_in_dim(weight_full, row_start, share_rows, 1)
    mode_count = sensitivity.shape[1]
    sens_share = lax.dynamic_slice_in_dim(
        sensitivity.reshape(mode_count, row_count), row_start, share_rows, 1
    )
    nominal_share = lax.dynamic_slice_in_dim(
        nominal_field.reshape(1, row_count), row_start, share_rows, 1
    )
    field_now = nominal_share + jnp.dot(aberrations, sens_share, preferred_element_type=jnp.float32)
    commands = initial_commands
    field_now = field_now + to_section_image(commands.astype(jnp.bfloat16), jac_block)
    for iteration in range(ITERS):
        residual = -back_of((weight * field_now).astype(jnp.bfloat16), jac_block)
        direction = residual
        change = jnp.zeros_like(residual)
        field_step = jnp.zeros_like(field_now)
        norm_now = reduce_scalars(jnp.sum(residual * residual, axis=1))
        for inner_step in range(CG):
            image_now = to_section_image(direction.astype(jnp.bfloat16), jac_block)
            applied = (
                back_of((weight * image_now).astype(jnp.bfloat16), jac_block)
                + regul[None, :] * direction
            )
            curvature = reduce_scalars(jnp.sum(direction * applied, axis=1))
            step_len = norm_now / (curvature + epsilon)
            residual = residual - step_len[:, None] * applied
            norm_next = reduce_scalars(jnp.sum(residual * residual, axis=1))
            change = change + step_len[:, None] * direction
            field_step = field_step + step_len[:, None] * image_now
            direction = residual + (norm_next / (norm_now + epsilon))[:, None] * direction
            norm_now = norm_next
        commands = commands + change
        field_now = field_now + field_step
    whole_field = lax.all_gather(
        field_now.astype(jnp.bfloat16), "section", axis=1, tiled=True
    ).astype(field_now.dtype)
    return (commands, whole_field.reshape(whole_field.shape[0], 1, components, pixels))


def control_kernel(
    n,
    rb,
    jac_hbm,
    base_ref,
    start_ref,
    regul_ref,
    weight_ref,
    cmd_ref,
    out_ref,
    jac,
    probe,
    masked,
    sec_part,
    sec_recv,
    wav_part,
    wav_recv,
    image,
    field,
    residual,
    direction,
    acc,
    applied_ref,
    dots_send,
    dots_recv,
    norm,
    steps,
    jac_sem,
    sec_ss,
    sec_rs,
    msk_ss,
    msk_rs,
    wav_ss,
    wav_rs,
    prb_ss,
    prb_rs,
    dot_ss,
    dot_rs,
    stp_ss,
    stp_rs,
):
    f32, bf16 = jnp.float32, jnp.bfloat16
    rows, acts = jac.shape
    reals = n * rb
    streams = range(STREAMS)
    rc, ac = rows // CHUNKS, acts // CHUNKS
    sec, wav = lax.axis_index("section"), lax.axis_index("wave")
    sec_peer = [lax.rem(sec + k, n) for k in range(1, n)]
    wav_peer = [lax.rem(wav + k, n) for k in range(1, n)]

    load = pltpu.make_async_copy(jac_hbm, jac, jac_sem)
    load.start()
    barrier = pltpu.get_barrier_semaphore()
    for p in sec_peer:
        pl.semaphore_signal(
            barrier, inc=1, device_id={"section": p}, device_id_type=pl.DeviceIdType.MESH
        )
    for p in wav_peer:
        pl.semaphore_signal(
            barrier, inc=1, device_id={"wave": p}, device_id_type=pl.DeviceIdType.MESH
        )
    pl.semaphore_wait(barrier, 2 * (n - 1))

    def to_section(k, src, dst, ss, rs):
        return pltpu.make_async_remote_copy(
            src_ref=src, dst_ref=dst, send_sem=ss, recv_sem=rs,
            device_id={"section": sec_peer[k]}, device_id_type=pl.DeviceIdType.MESH,
        )

    def to_wave(k, src, dst, ss, rs):
        return pltpu.make_async_remote_copy(
            src_ref=src, dst_ref=dst, send_sem=ss, recv_sem=rs,
            device_id={"wave": wav_peer[k]}, device_id_type=pl.DeviceIdType.MESH,
        )

    peers = range(n - 1)

    def sec_copy(h, j, k):
        return to_section(
            k, sec_part.at[h, j, sec_peer[k]], sec_recv.at[h, j, k], sec_ss.at[h, j, k], sec_rs.at[h, j, k]
        )

    def msk_copy(h, j, k):
        return to_section(
            k, masked.at[h, j, sec], masked.at[h, j, sec], msk_ss.at[h, j, k], msk_rs.at[h, j, k]
        )

    def wav_copy(h, c, k):
        return to_wave(
            k, wav_part.at[h, c, wav_peer[k]], wav_recv.at[h, c, k], wav_ss.at[h, c, k], wav_rs.at[h, c, k]
        )

    def prb_copy(h, slot, c, k):
        return to_wave(
            k,
            probe.at[slot, h, c, wav],
            probe.at[slot, h, c, wav],
            prb_ss.at[h, c, k],
            prb_rs.at[h, c, k],
        )

    def dot_copy(h, k):
        return to_section(k, dots_send.at[h], dots_recv.at[h, k], dot_ss.at[h, k], dot_rs.at[h, k])

    def stp_copy(h, k):
        return to_wave(k, steps.at[h, wav], steps.at[h, wav], stp_ss.at[h, k], stp_rs.at[h, k])

    def joined(blocks, width):
        return blocks.astype(f32).reshape(reals, width)

    def make_image(h, slot, arrive):
        for c in range(CHUNKS):
            arrive(c)
            lhs = joined(probe[slot, h, c], ac).astype(bf16)
            for j in range(CHUNKS):
                part = lax.dot_general(
                    lhs,
                    jac[j * rc:(j + 1) * rc, c * ac:(c + 1) * ac],
                    (((1,), (1,)), ((), ())),
                    preferred_element_type=f32,
                )
                if c:
                    part = acc[:, j * rc:(j + 1) * rc] + part
                if c < CHUNKS - 1:
                    acc[:, j * rc:(j + 1) * rc] = part
                else:
                    sec_part[h, j] = part.reshape(n, rb, rc).astype(bf16)
                    for k in peers:
                        sec_copy(h, j, k).start()

    def take_image(h, j):
        for k in peers:
            sec_copy(h, j, k).wait()
        total = sec_part[h, j, sec].astype(f32)
        for k in peers:
            total = total + sec_recv[h, j, k].astype(f32)
        return total

    def send_masked(h, j, values):
        masked[h, j, sec] = (weight_ref[:, j * rc:(j + 1) * rc] * values).astype(bf16)
        for k in peers:
            msk_copy(h, j, k).start()

    def make_back(h):
        for j in range(CHUNKS):
            for k in peers:
                msk_copy(h, j, k).wait()
            lhs = joined(masked[h, j], rc).astype(bf16)
            for c in range(CHUNKS):
                part = jnp.dot(
                    lhs,
                    jac[j * rc:(j + 1) * rc, c * ac:(c + 1) * ac],
                    preferred_element_type=f32,
                )
                if j:
                    part = acc[:, c * ac:(c + 1) * ac] + part
                if j < CHUNKS - 1:
                    acc[:, c * ac:(c + 1) * ac] = part
                else:
                    wav_part[h, c] = part.reshape(n, rb, ac).astype(bf16)
                    for k in peers:
                        wav_copy(h, c, k).start()

    def take_back(h, c):
        for k in peers:
            wav_copy(h, c, k).wait()
        total = wav_part[h, c, wav].astype(f32)
        for k in peers:
            total = total + wav_recv[h, c, k].astype(f32)
        return total

    lane = lax.broadcasted_iota(jnp.int32, (rb, LANES), 1)

    def send_dots(h, values):
        packed = jnp.zeros((rb, LANES), f32)
        for at, value in enumerate(values):
            packed = jnp.where(lane == at, value, packed)
        dots_send[h] = packed
        for k in peers:
            dot_copy(h, k).start()

    def take_dots(h, count):
        for k in peers:
            dot_copy(h, k).wait()
        total = dots_send[h]
        for k in peers:
            total = total + dots_recv[h, k]
        return [total[:, at:at + 1] for at in range(count)]

    def row_sum(values):
        return jnp.sum(values, axis=1, keepdims=True)

    def send_probe(h, slot, c, values):
        probe[slot, h, c, wav] = values.astype(bf16)
        for k in peers:
            prb_copy(h, slot, c, k).start()

    def take_steps(h, slot):
        for k in peers:
            stp_copy(h, k).wait()
        for j in range(CHUNKS):
            field[h, j] = field[h, j] + steps[h, sec][:, 0:1] * image[h, j]
        column = steps[h].reshape(reals, LANES)[:, 0:1]
        own = slice(h * reals, (h + 1) * reals)
        for c in range(CHUNKS):
            cols = slice(c * ac, (c + 1) * ac)
            cmd_ref[own, cols] = cmd_ref[own, cols] + column * joined(probe[slot, h, c], ac)

    cmd_ref[...] = start_ref[...]
    for h in streams:
        for c in range(CHUNKS):
            probe[0, h, c] = (
                start_ref[h * reals:(h + 1) * reals, c * ac:(c + 1) * ac]
                .reshape(n, rb, ac)
                .astype(bf16)
            )
    load.wait()
    for h in streams:
        make_image(h, 0, lambda c: None)
    for h in streams:
        for j in range(CHUNKS):
            field[h, j] = base_ref[h * rb:(h + 1) * rb, j * rc:(j + 1) * rc] + take_image(h, j)

    def iteration(_, carry):
        for h in streams:
            for j in range(CHUNKS):
                send_masked(h, j, field[h, j])
        for h in streams:
            make_back(h)
        for h in streams:
            square = jnp.zeros((rb, 1), f32)
            for c in range(CHUNKS):
                start = -take_back(h, c)
                residual[h, c] = start
                direction[h, c] = start
                send_probe(h, 0, c, start)
                square = square + row_sum(start * start)
            send_dots(h, [square])
        for h in streams:
            (first,) = take_dots(h, 1)
            norm[h] = jnp.broadcast_to(first, (rb, LANES))

        def cg_step(step, carry):
            slot = lax.rem(step, 2)

            for h in streams:

                def arrive(c):
                    for k in peers:
                        prb_copy(h, slot, c, k).wait()

                make_image(h, slot, arrive)

                @pl.when(step > 0)
                def _():
                    take_steps(h, 1 - slot)

            for h in streams:
                for j in range(CHUNKS):
                    total = take_image(h, j)
                    image[h, j] = total
                    send_masked(h, j, total)
            for h in streams:
                make_back(h)
            for h in streams:
                dd = jnp.zeros((rb, 1), f32)
                ra, aa = dd, dd
                for c in range(CHUNKS):
                    along = direction[h, c]
                    applied = take_back(h, c) + regul_ref[:, c * ac:(c + 1) * ac] * along
                    applied_ref[h, c] = applied
                    dd = dd + row_sum(along * applied)
                    ra = ra + row_sum(residual[h, c] * applied)
                    aa = aa + row_sum(applied * applied)
                send_dots(h, [dd, ra, aa])
            for h in streams:
                curvature, ra, aa = take_dots(h, 3)
                norm_now = norm[h][:, 0:1]
                step_len = norm_now / (curvature + epsilon)
                norm_next = jnp.maximum(norm_now + step_len * (step_len * aa - 2.0 * ra), 0.0)
                ratio = norm_next / (norm_now + epsilon)
                norm[h] = jnp.broadcast_to(norm_next, (rb, LANES))

                @pl.when(step < CG - 1)
                def _():
                    for c in range(CHUNKS):
                        after = residual[h, c] - step_len * applied_ref[h, c]
                        residual[h, c] = after
                        ahead = after + ratio * direction[h, c]
                        direction[h, c] = ahead
                        send_probe(h, 1 - slot, c, ahead)

                steps[h, wav] = jnp.broadcast_to(step_len, (rb, LANES))
                for k in peers:
                    stp_copy(h, k).start()

            return carry

        lax.fori_loop(0, CG, cg_step, 0)
        for h in streams:
            take_steps(h, (CG - 1) % 2)
        return carry

    lax.fori_loop(0, ITERS, iteration, 0)

    for h in streams:
        for j in range(CHUNKS):
            masked[h, j, sec] = field[h, j].astype(bf16)
            for k in peers:
                msk_copy(h, j, k).start()
    for h in streams:
        for j in range(CHUNKS):
            for k in peers:
                msk_copy(h, j, k).wait()
            out_ref[h * reals:(h + 1) * reals, j * rc:(j + 1) * rc] = joined(masked[h, j], rc)


def kernel_shards(nominal_field, sensitivity, aberrations, jacobian, tile_mask, regul, initial_commands):
    f32, bf16 = jnp.float32, jnp.bfloat16
    components, pixels, acts = jacobian.shape[1:]
    rows = components * pixels
    reals = initial_commands.shape[0]
    n = lax.axis_size("section")
    rb = reals // (n * STREAMS)
    rc, ac = rows // CHUNKS, acts // CHUNKS
    tile_count = tile_mask.shape[1]
    weight = jnp.broadcast_to(
        tile_mask[0].astype(f32)[None, :, None],
        (components, tile_count, pixels // tile_count),
    ).reshape(1, rows)
    own = lax.dynamic_index_in_dim(
        aberrations.reshape(STREAMS, n, rb, -1), lax.axis_index("section"), 1, keepdims=False
    ).reshape(STREAMS * rb, -1)
    base = nominal_field[0][None] + lax.dot_general(
        own, sensitivity[0], (((1,), (0,)), ((), ())), preferred_element_type=f32
    )
    vmem = pl.BlockSpec(memory_space=pltpu.VMEM)
    dma = pltpu.SemaphoreType.DMA
    commands, field = pl.pallas_call(
        functools.partial(control_kernel, n, rb),
        out_shape=(
            jax.ShapeDtypeStruct((reals, acts), f32),
            jax.ShapeDtypeStruct((reals, rows), f32),
        ),
        in_specs=[pl.BlockSpec(memory_space=pl.ANY), vmem, vmem, vmem, vmem],
        out_specs=(vmem, vmem),
        scratch_shapes=[
            pltpu.VMEM((rows, acts), bf16),
            pltpu.VMEM((2, STREAMS, CHUNKS, n, rb, ac), bf16),
            pltpu.VMEM((STREAMS, CHUNKS, n, rb, rc), bf16),
            pltpu.VMEM((STREAMS, CHUNKS, n, rb, rc), bf16),
            pltpu.VMEM((STREAMS, CHUNKS, n - 1, rb, rc), bf16),
            pltpu.VMEM((STREAMS, CHUNKS, n, rb, ac), bf16),
            pltpu.VMEM((STREAMS, CHUNKS, n - 1, rb, ac), bf16),
            pltpu.VMEM((STREAMS, CHUNKS, rb, rc), f32),
            pltpu.VMEM((STREAMS, CHUNKS, rb, rc), f32),
            pltpu.VMEM((STREAMS, CHUNKS, rb, ac), f32),
            pltpu.VMEM((STREAMS, CHUNKS, rb, ac), f32),
            pltpu.VMEM((n * rb, max(rows, acts)), f32),
            pltpu.VMEM((STREAMS, CHUNKS, rb, ac), f32),
            pltpu.VMEM((STREAMS, rb, LANES), f32),
            pltpu.VMEM((STREAMS, n - 1, rb, LANES), f32),
            pltpu.VMEM((STREAMS, rb, LANES), f32),
            pltpu.VMEM((STREAMS, n, rb, LANES), f32),
            dma(()),
        ]
        + [dma((STREAMS, CHUNKS, n - 1))] * 8
        + [dma((STREAMS, n - 1))] * 4,
        compiler_params=pltpu.CompilerParams(
            collective_id=0, has_side_effects=True, vmem_limit_bytes=40 * 1024 * 1024
        ),
        name="control_loop",
    )(
        jacobian.reshape(rows, acts),
        base.reshape(STREAMS * rb, rows),
        initial_commands,
        regul[None, :],
        weight,
    )
    return commands, field.reshape(reals, 1, components, pixels)


def solution(mesh):
    placed = (
        P("wave", None, None),
        P("wave", None, None, None),
        P("groups", None),
        P("wave", None, None, "section"),
        P("wave", None),
        P("section"),
        P("groups", "section"),
    )

    def choose(*args):
        n, waves = mesh.shape["section"], mesh.shape["wave"]
        reals = args[6].shape[0]
        acts = args[3].shape[3]
        rows = args[3].shape[1] * args[3].shape[2]
        fits = (
            n == waves
            and n > 1
            and reals % (8 * STREAMS * n) == 0
            and acts % (LANES * CHUNKS) == 0
            and rows % (LANES * CHUNKS) == 0
            and rows * acts <= 2048 * 2048
            and reals <= 64
        )
        return (kernel_shards if fits else general_shards)(*args)

    return jax.shard_map(
        choose,
        mesh=mesh,
        in_specs=placed,
        out_specs=(P("groups", "section"), P("groups", "wave", None, None)),
        check_vma=False,
    )
```

```python
import functools

import jax
import jax.numpy as jnp
from jax import lax
from jax.experimental import pallas as pl
from jax.experimental.pallas import tpu as pltpu
from jax.sharding import PartitionSpec as P

ITERS = 2
CG = 5
LANES = 128
CHUNKS = 2
STREAMS = 2

epsilon = 1e-06


def to_section_image(command_bf, jac_block):
    partial_value = lax.dot_general(
        command_bf, jac_block, (((1,), (1,)), ((), ())), preferred_element_type=jnp.float32
    )
    return lax.psum_scatter(
        partial_value.astype(jnp.bfloat16), "section", scatter_dimension=1, tiled=True
    ).astype(jnp.float32)


def back_of(masked_share, jac_block):
    masked_bf = lax.all_gather(masked_share, "section", axis=1, tiled=True)
    partial_value = jnp.dot(masked_bf, jac_block, preferred_element_type=jnp.float32)
    owned = lax.psum_scatter(
        partial_value.astype(jnp.bfloat16), "wave", scatter_dimension=1, tiled=True
    ).astype(jnp.float32)
    return lax.all_gather(owned, "wave", axis=1, tiled=True)


def reduce_scalars(values):
    return lax.psum(values, "section")


def general_shards(nominal_field, sensitivity, aberrations, jacobian, tile_mask, regul, initial_commands):
    components = jacobian.shape[1]
    pixels = jacobian.shape[2]
    block_width = jacobian.shape[3]
    row_count = components * pixels
    share_rows = row_count // lax.axis_size("section")
    row_start = lax.axis_index("section") * share_rows
    jac_block = jacobian.reshape(row_count, block_width)
    tile_count = tile_mask.shape[1]
    weight_full = jnp.broadcast_to(
        tile_mask[0].astype(jnp.float32)[None, :, None],
        (components, tile_count, pixels // tile_count),
    ).reshape(1, row_count)
    weight = lax.dynamic_slice_in_dim(weight_full, row_start, share_rows, 1)
    mode_count = sensitivity.shape[1]
    sens_share = lax.dynamic_slice_in_dim(
        sensitivity.reshape(mode_count, row_count), row_start, share_rows, 1
    )
    nominal_share = lax.dynamic_slice_in_dim(
        nominal_field.reshape(1, row_count), row_start, share_rows, 1
    )
    field_now = nominal_share + jnp.dot(aberrations, sens_share, preferred_element_type=jnp.float32)
    commands = initial_commands
    field_now = field_now + to_section_image(commands.astype(jnp.bfloat16), jac_block)
    for iteration in range(ITERS):
        residual = -back_of((weight * field_now).astype(jnp.bfloat16), jac_block)
        direction = residual
        change = jnp.zeros_like(residual)
        field_step = jnp.zeros_like(field_now)
        norm_now = reduce_scalars(jnp.sum(residual * residual, axis=1))
        for inner_step in range(CG):
            image_now = to_section_image(direction.astype(jnp.bfloat16), jac_block)
            applied = (
                back_of((weight * image_now).astype(jnp.bfloat16), jac_block)
                + regul[None, :] * direction
            )
            curvature = reduce_scalars(jnp.sum(direction * applied, axis=1))
            step_len = norm_now / (curvature + epsilon)
            residual = residual - step_len[:, None] * applied
            norm_next = reduce_scalars(jnp.sum(residual * residual, axis=1))
            change = change + step_len[:, None] * direction
            field_step = field_step + step_len[:, None] * image_now
            direction = residual + (norm_next / (norm_now + epsilon))[:, None] * direction
            norm_now = norm_next
        commands = commands + change
        field_now = field_now + field_step
    whole_field = lax.all_gather(
        field_now.astype(jnp.bfloat16), "section", axis=1, tiled=True
    ).astype(field_now.dtype)
    return (commands, whole_field.reshape(whole_field.shape[0], 1, components, pixels))


def control_kernel(
    n,
    rb,
    jac_hbm,
    base_ref,
    start_ref,
    regul_ref,
    weight_ref,
    cmd_ref,
    out_ref,
    jac,
    probe,
    masked,
    sec_part,
    sec_recv,
    wav_part,
    wav_recv,
    image,
    field,
    residual,
    direction,
    acc,
    applied_ref,
    dots_send,
    dots_recv,
    norm,
    steps,
    jac_sem,
    sec_ss,
    sec_rs,
    msk_ss,
    msk_rs,
    wav_ss,
    wav_rs,
    prb_ss,
    prb_rs,
    dot_ss,
    dot_rs,
    stp_ss,
    stp_rs,
):
    f32, bf16 = jnp.float32, jnp.bfloat16
    rows, acts = jac.shape
    reals = n * rb
    streams = range(STREAMS)
    rc, ac = rows // CHUNKS, acts // CHUNKS
    sec, wav = lax.axis_index("section"), lax.axis_index("wave")
    sec_peer = [lax.rem(sec + k, n) for k in range(1, n)]
    wav_peer = [lax.rem(wav + k, n) for k in range(1, n)]

    load = pltpu.make_async_copy(jac_hbm, jac, jac_sem)
    load.start()
    barrier = pltpu.get_barrier_semaphore()
    for p in sec_peer:
        pl.semaphore_signal(
            barrier, inc=1, device_id={"section": p}, device_id_type=pl.DeviceIdType.MESH
        )
    for p in wav_peer:
        pl.semaphore_signal(
            barrier, inc=1, device_id={"wave": p}, device_id_type=pl.DeviceIdType.MESH
        )
    pl.semaphore_wait(barrier, 2 * (n - 1))

    def to_section(k, src, dst, ss, rs):
        return pltpu.make_async_remote_copy(
            src_ref=src, dst_ref=dst, send_sem=ss, recv_sem=rs,
            device_id={"section": sec_peer[k]}, device_id_type=pl.DeviceIdType.MESH,
        )

    def to_wave(k, src, dst, ss, rs):
        return pltpu.make_async_remote_copy(
            src_ref=src, dst_ref=dst, send_sem=ss, recv_sem=rs,
            device_id={"wave": wav_peer[k]}, device_id_type=pl.DeviceIdType.MESH,
        )

    peers = range(n - 1)

    def sec_copy(h, j, k):
        return to_section(
            k, sec_part.at[h, j, sec_peer[k]], sec_recv.at[h, j, k], sec_ss.at[h, j, k], sec_rs.at[h, j, k]
        )

    def msk_copy(h, j, k):
        return to_section(
            k, masked.at[h, j, sec], masked.at[h, j, sec], msk_ss.at[h, j, k], msk_rs.at[h, j, k]
        )

    def wav_copy(h, c, k):
        return to_wave(
            k, wav_part.at[h, c, wav_peer[k]], wav_recv.at[h, c, k], wav_ss.at[h, c, k], wav_rs.at[h, c, k]
        )

    def prb_copy(h, slot, c, k):
        return to_wave(
            k,
            probe.at[slot, h, c, wav],
            probe.at[slot, h, c, wav],
            prb_ss.at[h, c, k],
            prb_rs.at[h, c, k],
        )

    def dot_copy(h, k):
        return to_section(k, dots_send.at[h], dots_recv.at[h, k], dot_ss.at[h, k], dot_rs.at[h, k])

    def stp_copy(h, k):
        return to_wave(k, steps.at[h, wav], steps.at[h, wav], stp_ss.at[h, k], stp_rs.at[h, k])

    def joined(blocks, width):
        return blocks.astype(f32).reshape(reals, width)

    def make_image(h, slot, arrive):
        for c in range(CHUNKS):
            arrive(c)
            lhs = joined(probe[slot, h, c], ac).astype(bf16)
            for j in range(CHUNKS):
                part = lax.dot_general(
                    lhs,
                    jac[j * rc:(j + 1) * rc, c * ac:(c + 1) * ac],
                    (((1,), (1,)), ((), ())),
                    preferred_element_type=f32,
                )
                if c:
                    part = acc[:, j * rc:(j + 1) * rc] + part
                if c < CHUNKS - 1:
                    acc[:, j * rc:(j + 1) * rc] = part
                else:
                    sec_part[h, j] = part.reshape(n, rb, rc).astype(bf16)
                    for k in peers:
                        sec_copy(h, j, k).start()

    def take_image(h, j):
        for k in peers:
            sec_copy(h, j, k).wait()
        total = sec_part[h, j, sec].astype(f32)
        for k in peers:
            total = total + sec_recv[h, j, k].astype(f32)
        return total

    def send_masked(h, j, values):
        masked[h, j, sec] = (weight_ref[:, j * rc:(j + 1) * rc] * values).astype(bf16)
        for k in peers:
            msk_copy(h, j, k).start()

    def make_back(h):
        for j in range(CHUNKS):
            for k in peers:
                msk_copy(h, j, k).wait()
            lhs = joined(masked[h, j], rc).astype(bf16)
            for c in range(CHUNKS):
                part = jnp.dot(
                    lhs,
                    jac[j * rc:(j + 1) * rc, c * ac:(c + 1) * ac],
                    preferred_element_type=f32,
                )
                if j:
                    part = acc[:, c * ac:(c + 1) * ac] + part
                if j < CHUNKS - 1:
                    acc[:, c * ac:(c + 1) * ac] = part
                else:
                    wav_part[h, c] = part.reshape(n, rb, ac).astype(bf16)
                    for k in peers:
                        wav_copy(h, c, k).start()

    def take_back(h, c):
        for k in peers:
            wav_copy(h, c, k).wait()
        total = wav_part[h, c, wav].astype(f32)
        for k in peers:
            total = total + wav_recv[h, c, k].astype(f32)
        return total

    lane = lax.broadcasted_iota(jnp.int32, (rb, LANES), 1)

    def send_dots(h, values):
        packed = jnp.zeros((rb, LANES), f32)
        for at, value in enumerate(values):
            packed = jnp.where(lane == at, value, packed)
        dots_send[h] = packed
        for k in peers:
            dot_copy(h, k).start()

    def take_dots(h, count):
        for k in peers:
            dot_copy(h, k).wait()
        total = dots_send[h]
        for k in peers:
            total = total + dots_recv[h, k]
        return [total[:, at:at + 1] for at in range(count)]

    def row_sum(values):
        return jnp.sum(values, axis=1, keepdims=True)

    def send_probe(h, slot, c, values):
        probe[slot, h, c, wav] = values.astype(bf16)
        for k in peers:
            prb_copy(h, slot, c, k).start()

    def take_steps(h, slot):
        for k in peers:
            stp_copy(h, k).wait()
        for j in range(CHUNKS):
            field[h, j] = field[h, j] + steps[h, sec][:, 0:1] * image[h, j]
        column = steps[h].reshape(reals, LANES)[:, 0:1]
        own = slice(h * reals, (h + 1) * reals)
        for c in range(CHUNKS):
            cols = slice(c * ac, (c + 1) * ac)
            cmd_ref[own, cols] = cmd_ref[own, cols] + column * joined(probe[slot, h, c], ac)

    cmd_ref[...] = start_ref[...]
    for h in streams:
        for c in range(CHUNKS):
            probe[0, h, c] = (
                start_ref[h * reals:(h + 1) * reals, c * ac:(c + 1) * ac]
                .reshape(n, rb, ac)
                .astype(bf16)
            )
    load.wait()
    for h in streams:
        make_image(h, 0, lambda c: None)
    for h in streams:
        for j in range(CHUNKS):
            field[h, j] = base_ref[h * rb:(h + 1) * rb, j * rc:(j + 1) * rc] + take_image(h, j)

    def iteration(_, carry):
        for h in streams:
            for j in range(CHUNKS):
                send_masked(h, j, field[h, j])
        for h in streams:
            make_back(h)
        for h in streams:
            square = jnp.zeros((rb, 1), f32)
            for c in range(CHUNKS):
                start = -take_back(h, c)
                residual[h, c] = start
                direction[h, c] = start
                send_probe(h, 0, c, start)
                square = square + row_sum(start * start)
            send_dots(h, [square])
        for h in streams:
            (first,) = take_dots(h, 1)
            norm[h] = jnp.broadcast_to(first, (rb, LANES))

        def cg_step(step, carry):
            slot = lax.rem(step, 2)

            for h in streams:

                def arrive(c):
                    for k in peers:
                        prb_copy(h, slot, c, k).wait()

                make_image(h, slot, arrive)

            @pl.when(step > 0)
            def _():
                for h in streams:
                    take_steps(h, 1 - slot)

            for h in streams:
                for j in range(CHUNKS):
                    total = take_image(h, j)
                    image[h, j] = total
                    send_masked(h, j, total)
            for h in streams:
                make_back(h)
            for h in streams:
                dd = jnp.zeros((rb, 1), f32)
                ra, aa = dd, dd
                for c in range(CHUNKS):
                    along = direction[h, c]
                    applied = take_back(h, c) + regul_ref[:, c * ac:(c + 1) * ac] * along
                    applied_ref[h, c] = applied
                    dd = dd + row_sum(along * applied)
                    ra = ra + row_sum(residual[h, c] * applied)
                    aa = aa + row_sum(applied * applied)
                send_dots(h, [dd, ra, aa])
            for h in streams:
                curvature, ra, aa = take_dots(h, 3)
                norm_now = norm[h][:, 0:1]
                step_len = norm_now / (curvature + epsilon)
                norm_next = jnp.maximum(norm_now + step_len * (step_len * aa - 2.0 * ra), 0.0)
                ratio = norm_next / (norm_now + epsilon)
                norm[h] = jnp.broadcast_to(norm_next, (rb, LANES))

                @pl.when(step < CG - 1)
                def _():
                    for c in range(CHUNKS):
                        after = residual[h, c] - step_len * applied_ref[h, c]
                        residual[h, c] = after
                        ahead = after + ratio * direction[h, c]
                        direction[h, c] = ahead
                        send_probe(h, 1 - slot, c, ahead)

                steps[h, wav] = jnp.broadcast_to(step_len, (rb, LANES))
                for k in peers:
                    stp_copy(h, k).start()

            return carry

        lax.fori_loop(0, CG, cg_step, 0)
        for h in streams:
            take_steps(h, (CG - 1) % 2)
        return carry

    lax.fori_loop(0, ITERS, iteration, 0)

    for h in streams:
        for j in range(CHUNKS):
            masked[h, j, sec] = field[h, j].astype(bf16)
            for k in peers:
                msk_copy(h, j, k).start()
    for h in streams:
        for j in range(CHUNKS):
            for k in peers:
                msk_copy(h, j, k).wait()
            out_ref[h * reals:(h + 1) * reals, j * rc:(j + 1) * rc] = joined(masked[h, j], rc)


def kernel_shards(nominal_field, sensitivity, aberrations, jacobian, tile_mask, regul, initial_commands):
    f32, bf16 = jnp.float32, jnp.bfloat16
    components, pixels, acts = jacobian.shape[1:]
    rows = components * pixels
    reals = initial_commands.shape[0]
    n = lax.axis_size("section")
    rb = reals // (n * STREAMS)
    rc, ac = rows // CHUNKS, acts // CHUNKS
    tile_count = tile_mask.shape[1]
    weight = jnp.broadcast_to(
        tile_mask[0].astype(f32)[None, :, None],
        (components, tile_count, pixels // tile_count),
    ).reshape(1, rows)
    own = lax.dynamic_index_in_dim(
        aberrations.reshape(STREAMS, n, rb, -1), lax.axis_index("section"), 1, keepdims=False
    ).reshape(STREAMS * rb, -1)
    base = nominal_field[0][None] + lax.dot_general(
        own, sensitivity[0], (((1,), (0,)), ((), ())), preferred_element_type=f32
    )
    vmem = pl.BlockSpec(memory_space=pltpu.VMEM)
    dma = pltpu.SemaphoreType.DMA
    commands, field = pl.pallas_call(
        functools.partial(control_kernel, n, rb),
        out_shape=(
            jax.ShapeDtypeStruct((reals, acts), f32),
            jax.ShapeDtypeStruct((reals, rows), f32),
        ),
        in_specs=[pl.BlockSpec(memory_space=pl.ANY), vmem, vmem, vmem, vmem],
        out_specs=(vmem, vmem),
        scratch_shapes=[
            pltpu.VMEM((rows, acts), bf16),
            pltpu.VMEM((2, STREAMS, CHUNKS, n, rb, ac), bf16),
            pltpu.VMEM((STREAMS, CHUNKS, n, rb, rc), bf16),
            pltpu.VMEM((STREAMS, CHUNKS, n, rb, rc), bf16),
            pltpu.VMEM((STREAMS, CHUNKS, n - 1, rb, rc), bf16),
            pltpu.VMEM((STREAMS, CHUNKS, n, rb, ac), bf16),
            pltpu.VMEM((STREAMS, CHUNKS, n - 1, rb, ac), bf16),
            pltpu.VMEM((STREAMS, CHUNKS, rb, rc), f32),
            pltpu.VMEM((STREAMS, CHUNKS, rb, rc), f32),
            pltpu.VMEM((STREAMS, CHUNKS, rb, ac), f32),
            pltpu.VMEM((STREAMS, CHUNKS, rb, ac), f32),
            pltpu.VMEM((n * rb, max(rows, acts)), f32),
            pltpu.VMEM((STREAMS, CHUNKS, rb, ac), f32),
            pltpu.VMEM((STREAMS, rb, LANES), f32),
            pltpu.VMEM((STREAMS, n - 1, rb, LANES), f32),
            pltpu.VMEM((STREAMS, rb, LANES), f32),
            pltpu.VMEM((STREAMS, n, rb, LANES), f32),
            dma(()),
        ]
        + [dma((STREAMS, CHUNKS, n - 1))] * 8
        + [dma((STREAMS, n - 1))] * 4,
        compiler_params=pltpu.CompilerParams(
            collective_id=0, has_side_effects=True, vmem_limit_bytes=40 * 1024 * 1024
        ),
        name="control_loop",
    )(
        jacobian.reshape(rows, acts),
        base.reshape(STREAMS * rb, rows),
        initial_commands,
        regul[None, :],
        weight,
    )
    return commands, field.reshape(reals, 1, components, pixels)


def solution(mesh):
    placed = (
        P("wave", None, None),
        P("wave", None, None, None),
        P("groups", None),
        P("wave", None, None, "section"),
        P("wave", None),
        P("section"),
        P("groups", "section"),
    )

    def choose(*args):
        n, waves = mesh.shape["section"], mesh.shape["wave"]
        reals = args[6].shape[0]
        acts = args[3].shape[3]
        rows = args[3].shape[1] * args[3].shape[2]
        fits = (
            n == waves
            and n > 1
            and reals % (8 * STREAMS * n) == 0
            and acts % (LANES * CHUNKS) == 0
            and rows % (LANES * CHUNKS) == 0
            and rows * acts <= 2048 * 2048
            and reals <= 64
        )
        return (kernel_shards if fits else general_shards)(*args)

    return jax.shard_map(
        choose,
        mesh=mesh,
        in_specs=placed,
        out_specs=(P("groups", "section"), P("groups", "wave", None, None)),
        check_vma=False,
    )
```
